256 devices in a mesh: dp: 32 (over x, y, core), mp: 8 (over z).
Axes of the slice: x: 4, y: 4, z: 8, core: 2. Of those that a mesh axis runs over, the one named last changes fastest.
Arguments:
- query_rows: bfloat16 [32768, 5120], P('dp', 'mp'), may hold values from -160 to 160
- key_rows: bfloat16 [32768, 1024], P('dp', 'mp'), may hold values from -8 to 8
- value_rows: bfloat16 [32768, 1024], P('dp', 'mp'), may hold values from -6 to 6
- grad_out: bfloat16 [32768, 5120], P('dp', 'mp'), may hold values from -6 to 6
- out_proj: bfloat16 [5120, 5120], P('mp'), may hold values from -0.078125 to 0.078125
- lengths: int32 [512, 4], replicated, may hold values from 1 to 48, 64 in all within a row
- offsets: int32 [16], replicated, may hold values from 0 to 31, as said below
Outputs:
- grad_query: bfloat16 [32768, 5120], P('dp', 'mp')
- grad_key: bfloat16 [32768, 1024], P('dp', 'mp')
- grad_value: bfloat16 [32768, 1024], P('dp', 'mp')
- grad_proj: float32 [5120, 5120], P('dp', 'mp')
The draws below stay inside these ranges and needn't reach their ends.
Inputs may be any that keep to these rules, and one draw needn't show every extreme that they name: Each row is the document lengths of one block, summing to 64; the longest is exactly 48. `offsets`: the 16 values are distinct.
All inputs are finite; a program needn't handle non-finite values.
Results may differ from the reference program's by a relative error of at most 0.033.
Values may be sent and summed in bfloat16 or wider, within the bound.
No kernel may reach another device: no remote copies, remote signals or barrier semaphores. Data moves between devices by JAX's collectives and lax.ppermute only.
A program may use at most 128 MiB of HBM per device.

```python
import math
import jax
import jax.numpy as jnp
import numpy as np
from jax import lax

D = 5120
HEADS = 40
KVH = 8
HD = 128
BLOCK = 64
NCH = 16
NDOC = 4
MOST = 48
NCHUNKS = 512
TOKENS = 32768
N_DP = 32


def joint_draw(key):
    base = jax.random.fold_in(key, 4242)
    first, second = jax.random.split(base, 2)
    key_vals = jax.random.truncated_normal(first, -6.0, 6.0, (TOKENS, KVH * HD), jnp.float32)
    query_vals = jax.random.truncated_normal(second, -6.0, 6.0, (TOKENS, HEADS * HD), jnp.float32)
    return (query_vals, key_vals)


def draw_query_rows(key, part):
    query_vals, key_vals = joint_draw(key)
    return query_vals.astype(jnp.bfloat16)


def draw_key_rows(key, part):
    query_vals, key_vals = joint_draw(key)
    return key_vals.astype(jnp.bfloat16)


def draw_offsets(key, part):
    middle = (jax.random.permutation(jax.random.fold_in(key, 99), N_DP - 2) + 1).astype(jnp.int32)
    listed = jnp.concatenate([jnp.full((1,), N_DP - 1, jnp.int32), jnp.zeros((1,), jnp.int32), middle])
    picks = listed[:NCH]
    order = jax.random.permutation(jax.random.fold_in(key, 98), NCH)
    return picks[order].astype(jnp.int32)


def raised(array, key, source, target, blocks, factor):
    owner, partner = [(jnp.arange(array.shape[dim]) // (array.shape[dim] // blocks)).reshape([-1 if axis == dim else 1 for axis in range(array.ndim)]) for dim in (source, target)]
    chosen = jax.random.permutation(key, blocks)[partner]
    strong = (owner == chosen) | (owner == (partner + blocks // 2) % blocks)
    return jnp.where(strong, factor * array, array)


def steps_of(stream_key, dims, shards, least, top_value):
    factor_of = 1.0
    for dim, blocks in shards:
        steps = jax.random.uniform(jax.random.fold_in(jax.random.fold_in(stream_key, 6), dim), (blocks,), jnp.float32, least / len(shards), top_value / len(shards))
        factor_of = factor_of * jnp.repeat(jnp.exp(steps), dims[dim] // blocks).reshape((-1,) + (1,) * (len(dims) - 1 - dim))
    return factor_of


def split_up(amount, total, bound, skew):
    portions = [(1 << 20) // math.isqrt(standing ** skew) + 1 for standing in range(2, amount + 1)]
    surplus, counts = total - bound - (amount - 1), [1] * (amount - 1)
    while surplus > 0:
        candidates = [i for i in range(amount - 1) if counts[i] < bound]
        whole, budget = sum([portions[i] for i in candidates]), surplus
        for i in candidates:
            extra = min(bound - counts[i], max(1, budget * portions[i] // whole), surplus)
            counts[i] = counts[i] + extra
            surplus = surplus - extra
    return np.array([bound] + counts)


def uneven(stream_key, amount, total, bound, skew):
    if amount == 2:
        one = jax.random.randint(stream_key, (), max(1, total - bound), min(bound, total - 1) + 1)
        return jnp.stack([one, total - one])
    tallies = jnp.asarray(split_up(amount, total, bound, skew), jnp.int32)
    pairs = (amount - 1) // 2
    donor, receiver = tallies[1:1 + 2 * pairs:2], tallies[2:2 + 2 * pairs:2]
    slack = jnp.minimum(donor - 1, bound - receiver)
    moved = jax.random.randint(jax.random.fold_in(stream_key, 1), (pairs,), 0, 1 << 20) % (slack + 1)
    tallies = tallies.at[1:1 + 2 * pairs:2].set(donor - moved).at[2:2 + 2 * pairs:2].set(receiver + moved)
    return tallies[jax.random.permutation(jax.random.fold_in(stream_key, 2), amount)]


def noise(stream_key, extent, spread, most, cuts=(), kind=jnp.bfloat16):
    entries = spread * jax.random.normal(stream_key, extent, jnp.float32)
    if cuts:
        entries = entries * steps_of(stream_key, extent, cuts, -0.22, 0.18)
    return jnp.clip(entries, -most, most).astype(kind)


def heavy_noise(stream_key, dims, spread, bound, pieces, heavy, kind=jnp.bfloat16):
    drawn = spread * jax.random.normal(stream_key, dims, jnp.float32)
    if pieces:
        drawn = drawn * steps_of(stream_key, dims, pieces, -0.22, 0.18)
    return jnp.clip(raised(drawn, jax.random.fold_in(stream_key, 3), *heavy), -bound, bound).astype(kind)


def setup_inputs(seed: int = 0) -> dict:
    splits = jax.random.split(jax.random.key(seed), 8)
    query_rows = draw_query_rows(jax.random.fold_in(splits[7], 71), 0)
    key_rows = draw_key_rows(jax.random.fold_in(splits[7], 71), 0)
    value_rows = noise(splits[2], (TOKENS, KVH * HD), 1.0, 6.0, ((0, 32), (1, 8)))
    grad_out = heavy_noise(splits[3], (TOKENS, D), 1.0, 6.0, ((0, 32), (1, 8)), (0, 1, 32, 2.75))
    out_proj = noise(splits[4], (HEADS * HD, D), (HEADS * HD) ** -0.5, 0.078125, ((0, 8),))
    lengths = jax.vmap(lambda own: uneven(own, NDOC, BLOCK, MOST, 2))(jax.random.split(splits[5], NCHUNKS)).reshape((NCHUNKS, NDOC)).astype(jnp.int32)
    offsets = draw_offsets(jax.random.fold_in(splits[7], 71), 0)
    return {"query_rows": query_rows, "key_rows": key_rows, "value_rows": value_rows, "grad_out": grad_out, "out_proj": out_proj, "lengths": lengths, "offsets": offsets}


def doc_layout(lengths, block_len):
    doc_ends = jnp.cumsum(lengths, axis=1).astype(jnp.int32)
    positions = jnp.arange(block_len, dtype=jnp.int32)
    segment = jnp.sum((doc_ends[:, None, :] <= positions[None, :, None]).astype(jnp.int32), axis=2).astype(jnp.int32)
    doc_ids = jnp.arange(lengths.shape[1], dtype=jnp.int32)
    onehot_doc = segment[:, :, None] == doc_ids[None, None, :]
    own_length = jnp.sum(jnp.where(onehot_doc, lengths[:, None, :], 0), axis=2)
    token_weight = 1.0 / own_length.astype(jnp.float32)
    return segment, token_weight


def block_grads(query_blk, key_blk, value_blk, grad_blk, segment):
    length = query_blk.shape[0]
    scaling = query_blk.shape[-1] ** -0.5
    positions = jnp.arange(length, dtype=jnp.int32)
    allowed = (segment[:, None] == segment[None, :]) & (positions[None, :] <= positions[:, None])
    query_float = query_blk.astype(jnp.float32)
    key_float = key_blk.astype(jnp.float32)
    value_float = value_blk.astype(jnp.float32)
    grad_float = grad_blk.astype(jnp.float32)
    scores = jnp.einsum("qkgd,pkd->kgqp", query_float, key_float) * scaling
    scores = jnp.where(allowed[None, None], scores, -1e30)
    top_score = jnp.max(scores, axis=-1, keepdims=True)
    exponent = jnp.where(allowed[None, None], jnp.exp(scores - top_score), 0.0)
    denominator = jnp.sum(exponent, axis=-1, keepdims=True)
    soft = exponent / denominator
    soft_weight = soft.astype(jnp.bfloat16)
    attended = jnp.einsum("kgqp,pkd->qkgd", soft_weight.astype(jnp.float32), value_float).astype(jnp.bfloat16)
    row_dot = jnp.sum(grad_float * attended.astype(jnp.float32), axis=-1)
    grad_soft = jnp.einsum("qkgd,pkd->kgqp", grad_float, value_float)
    grad_score = (soft * (grad_soft - jnp.transpose(row_dot, (1, 2, 0))[..., None])).astype(jnp.bfloat16)
    score_float = grad_score.astype(jnp.float32)
    grad_q = (jnp.einsum("kgqp,pkd->qkgd", score_float, key_float) * scaling).astype(jnp.bfloat16)
    grad_k = (jnp.einsum("kgqp,qkgd->pkd", score_float, query_float) * scaling).astype(jnp.bfloat16)
    grad_v = jnp.einsum("kgqp,qkgd->pkd", soft_weight.astype(jnp.float32), grad_float).astype(jnp.bfloat16)
    return attended, grad_q, grad_k, grad_v


def reference(query_rows, key_rows, value_rows, grad_out, out_proj, lengths, offsets):
    segment, token_weight = doc_layout(lengths, BLOCK)
    weighted = (grad_out.astype(jnp.float32) * token_weight.reshape(-1, 1)).astype(jnp.bfloat16)
    head_grad = lax.dot_general(weighted, out_proj, (((1,), (1,)), ((), ())), preferred_element_type=jnp.float32).astype(jnp.bfloat16)
    ranks = jnp.arange(N_DP, dtype=jnp.int32)
    slot_ids = jnp.arange(NCH, dtype=jnp.int32)
    sources = ((((ranks[:, None] - offsets[None, :]) % N_DP) * NCH) + slot_ids[None, :]).reshape(-1).astype(jnp.int32)
    group = HEADS // KVH

    def moved(matrix):
        return matrix.reshape(NCHUNKS, BLOCK, matrix.shape[1])[sources]

    query_moved = moved(query_rows).reshape(NCHUNKS, BLOCK, KVH, group, HD)
    key_moved = moved(key_rows).reshape(NCHUNKS, BLOCK, KVH, HD)
    value_moved = moved(value_rows).reshape(NCHUNKS, BLOCK, KVH, HD)
    grad_moved = moved(head_grad).reshape(NCHUNKS, BLOCK, KVH, group, HD)
    segment_moved = segment[sources]

    def one_block(items):
        return block_grads(items[0], items[1], items[2], items[3], items[4])

    attended, grad_q, grad_k, grad_v = lax.map(one_block, (query_moved, key_moved, value_moved, grad_moved, segment_moved))
    weighted_moved = moved(weighted).reshape(TOKENS, D)
    grad_proj = lax.dot_general(weighted_moved, attended.reshape(TOKENS, HEADS * HD), (((0,), (0,)), ((), ())), preferred_element_type=jnp.float32)
    return (grad_q.reshape(TOKENS, HEADS * HD), grad_k.reshape(TOKENS, KVH * HD), grad_v.reshape(TOKENS, KVH * HD), grad_proj)
```

```python
import jax
import jax.numpy as jnp
from jax import lax
from jax.experimental import pallas as pl
from jax.experimental.pallas import tpu as pltpu
from jax.sharding import Mesh, PartitionSpec as P


HEADS = 40
KVH = 8
HD = 128
GROUP = HEADS // KVH
BLOCK = 64
HALF = BLOCK // 2
SLOTS = 16
RANKS = 32
QW = GROUP * HD
SENT = QW + 2 * HD
PACK = 4
ROWS = PACK * HALF
SCALE = HD**-0.5
F32 = jnp.float32
BF16 = jnp.bfloat16

NT = (((1,), (1,)), ((), ()))
TN = (((0,), (0,)), ((), ()))
NN = (((1,), (0,)), ((), ()))


def mm(a, b, dims):
    return lax.dot_general(a, b, dims, preferred_element_type=F32)


def doc_layout(lengths, block_len):
    doc_ends = jnp.cumsum(lengths, axis=1)
    positions = jnp.arange(block_len, dtype=jnp.int32)
    segment = jnp.sum((doc_ends[:, None, :] <= positions[None, :, None]).astype(jnp.int32), axis=2)
    doc_ids = jnp.arange(lengths.shape[1], dtype=jnp.int32)
    onehot_doc = segment[:, :, None] == doc_ids[None, None, :]
    own_length = jnp.sum(jnp.where(onehot_doc, lengths[:, None, :], 0), axis=2)
    return segment, 1.0 / own_length.astype(F32)


def halves(ref):
    x = ref[...]
    return x[:, :HALF].reshape(ROWS, x.shape[2]), x[:, HALF:].reshape(ROWS, x.shape[2])


def lower_mask():
    r = lax.broadcasted_iota(jnp.int32, (ROWS, ROWS), 0)
    c = lax.broadcasted_iota(jnp.int32, (ROWS, ROWS), 1)
    return c <= r


def forward_kernel(q_ref, k_ref, v_ref, rows0_ref, rows1_ref, cols0_ref, cols1_ref, att0_ref, att1_ref, s00_ref, s10_ref, s11_ref):
    q0, q1 = halves(q_ref)
    k0, k1 = halves(k_ref)
    v0, v1 = halves(v_ref)
    rows0, rows1 = rows0_ref[...], rows1_ref[...]
    cols0, cols1 = cols0_ref[0], cols1_ref[0]
    low = lower_mask()
    m00 = (rows0 == cols0) & low
    m10 = rows1 == cols0
    m11 = (rows1 == cols1) & low
    for h in range(GROUP):
        cut = slice(h * HD, (h + 1) * HD)
        qh = q0[:, cut]
        s = jnp.where(m00, mm(qh, k0, NT) * SCALE, -1e30)
        e = jnp.where(m00, jnp.exp(s - jnp.max(s, axis=1, keepdims=True)), 0.0)
        soft = e / jnp.sum(e, axis=1, keepdims=True)
        s00_ref[0, h] = soft
        att0_ref[:, cut] = mm(soft.astype(BF16), v0, NN).astype(BF16)
        qh = q1[:, cut]
        s0 = jnp.where(m10, mm(qh, k0, NT) * SCALE, -1e30)
        s1 = jnp.where(m11, mm(qh, k1, NT) * SCALE, -1e30)
        top = jnp.maximum(jnp.max(s0, axis=1, keepdims=True), jnp.max(s1, axis=1, keepdims=True))
        e0 = jnp.where(m10, jnp.exp(s0 - top), 0.0)
        e1 = jnp.where(m11, jnp.exp(s1 - top), 0.0)
        total = jnp.sum(e0, axis=1, keepdims=True) + jnp.sum(e1, axis=1, keepdims=True)
        soft0, soft1 = e0 / total, e1 / total
        s10_ref[0, h] = soft0
        s11_ref[0, h] = soft1
        att1_ref[:, cut] = (mm(soft0.astype(BF16), v0, NN) + mm(soft1.astype(BF16), v1, NN)).astype(BF16)


def id_views(ids):
    half = ids.reshape(SLOTS, 2, HALF)
    id0, id1 = half[:, 0].reshape(-1), half[:, 1].reshape(-1)
    steps = SLOTS // PACK
    return id0[:, None], id1[:, None], id0.reshape(steps, 1, ROWS), id1.reshape(steps, 1, ROWS)


def forward(q, k, v, *id_arrays):
    steps = SLOTS // PACK
    wide = lambda n: pl.BlockSpec((PACK, BLOCK, n), lambda i: (i, 0, 0))
    rows = pl.BlockSpec((ROWS, 1), lambda i: (i, 0))
    cols = pl.BlockSpec((1, 1, ROWS), lambda i: (i, 0, 0))
    att = pl.BlockSpec((ROWS, QW), lambda i: (i, 0))
    soft = pl.BlockSpec((1, GROUP, ROWS, ROWS), lambda i: (i, 0, 0, 0))
    return pl.pallas_call(
        forward_kernel,
        grid=(steps,),
        in_specs=[wide(QW), wide(HD), wide(HD), rows, rows, cols, cols],
        out_specs=[att, att, soft, soft, soft],
        out_shape=[jax.ShapeDtypeStruct((SLOTS * HALF, QW), BF16)] * 2
        + [jax.ShapeDtypeStruct((steps, GROUP, ROWS, ROWS), F32)] * 3,
        name="forward",
        cost_estimate=pl.CostEstimate(flops=10**9, bytes_accessed=10**7, transcendentals=10**6),
    )(
        q.reshape(SLOTS, BLOCK, QW),
        k.reshape(SLOTS, BLOCK, HD),
        v.reshape(SLOTS, BLOCK, HD),
        *id_arrays,
    )


def put(send_ref, tgt_ref, first, value, lo):
    for j in range(PACK):
        send_ref[tgt_ref[first + j], :, lo : lo + value.shape[1]] = value[j * HALF : (j + 1) * HALF].astype(BF16)


def late_kernel(tgt_ref, hg_ref, att_ref, q_ref, k_ref, v_ref, s10_ref, s11_ref, send_ref, dk_ref, dv_ref):
    first = pl.program_id(0) * PACK
    q1 = halves(q_ref)[1]
    k0, k1 = halves(k_ref)
    v0, v1 = halves(v_ref)
    dk0 = dk1 = dv0 = dv1 = jnp.zeros((ROWS, HD), F32)
    for h in range(GROUP):
        cut = slice(h * HD, (h + 1) * HD)
        g, qh = hg_ref[:, cut], q1[:, cut]
        soft0, soft1 = s10_ref[0, h], s11_ref[0, h]
        dot = jnp.sum(g.astype(F32) * att_ref[:, cut].astype(F32), axis=1, keepdims=True)
        d0 = (soft0 * (mm(g, v0, NT) - dot)).astype(BF16)
        d1 = (soft1 * (mm(g, v1, NT) - dot)).astype(BF16)
        put(send_ref, tgt_ref, first, (mm(d0, k0, NN) + mm(d1, k1, NN)) * SCALE, h * HD)
        dk0 += mm(d0, qh, TN)
        dk1 += mm(d1, qh, TN)
        dv0 += mm(soft0.astype(BF16), g, TN)
        dv1 += mm(soft1.astype(BF16), g, TN)
    put(send_ref, tgt_ref, first, dk1 * SCALE, QW)
    put(send_ref, tgt_ref, first, dv1, QW + HD)
    dk_ref[...] = dk0
    dv_ref[...] = dv0


def early_kernel(tgt_ref, hg_ref, att_ref, q_ref, k_ref, v_ref, s00_ref, dk_ref, dv_ref, send_ref):
    first = pl.program_id(0) * PACK
    q0 = halves(q_ref)[0]
    k0 = halves(k_ref)[0]
    v0 = halves(v_ref)[0]
    dk0, dv0 = dk_ref[...], dv_ref[...]
    for h in range(GROUP):
        cut = slice(h * HD, (h + 1) * HD)
        g, qh = hg_ref[:, cut], q0[:, cut]
        soft0 = s00_ref[0, h]
        dot = jnp.sum(g.astype(F32) * att_ref[:, cut].astype(F32), axis=1, keepdims=True)
        d0 = (soft0 * (mm(g, v0, NT) - dot)).astype(BF16)
        put(send_ref, tgt_ref, first, mm(d0, k0, NN) * SCALE, h * HD)
        dk0 += mm(d0, qh, TN)
        dv0 += mm(soft0.astype(BF16), g, TN)
    put(send_ref, tgt_ref, first, dk0 * SCALE, QW)
    put(send_ref, tgt_ref, first, dv0, QW + HD)


def backward(late, targets, hg, att, q, k, v, softs, carry=()):
    wide = lambda n: pl.BlockSpec((PACK, BLOCK, n), lambda i, t: (i, 0, 0))
    att_spec = pl.BlockSpec((ROWS, QW), lambda i, t: (i, 0))
    soft = pl.BlockSpec((1, GROUP, ROWS, ROWS), lambda i, t: (i, 0, 0, 0))
    narrow = pl.BlockSpec((ROWS, HD), lambda i, t: (i, 0))
    send = pl.BlockSpec((RANKS, HALF, SENT), lambda i, t: (0, 0, 0))
    send_shape = jax.ShapeDtypeStruct((RANKS, HALF, SENT), BF16)
    part = jax.ShapeDtypeStruct((SLOTS * HALF, HD), F32)
    return pl.pallas_call(
        late_kernel if late else early_kernel,
        grid_spec=pltpu.PrefetchScalarGridSpec(
            num_scalar_prefetch=1,
            grid=(SLOTS // PACK,),
            in_specs=[att_spec, att_spec, wide(QW), wide(HD), wide(HD)] + [soft] * len(softs) + [narrow] * len(carry),
            out_specs=[send, narrow, narrow] if late else send,
        ),
        out_shape=[send_shape, part, part] if late else send_shape,
        name="late" if late else "early",
        cost_estimate=pl.CostEstimate(flops=10**9, bytes_accessed=10**7, transcendentals=0),
    )(
        targets,
        hg,
        att,
        q.reshape(SLOTS, BLOCK, QW),
        k.reshape(SLOTS, BLOCK, HD),
        v.reshape(SLOTS, BLOCK, HD),
        *softs,
        *carry,
    )


def collect_kernel(src_ref, early_ref, late_ref, gq_ref, gk_ref, gv_ref):
    for s in range(SLOTS):
        for ref, lo in ((early_ref, s * BLOCK), (late_ref, s * BLOCK + HALF)):
            rows = pl.ds(lo, HALF)
            piece = ref[src_ref[s]]
            gq_ref[rows] = piece[:, :QW]
            gk_ref[rows] = piece[:, QW : QW + HD]
            gv_ref[rows] = piece[:, QW + HD :]


def collect(sources, early, late):
    n = SLOTS * BLOCK
    whole = pl.BlockSpec(memory_space=pltpu.VMEM)
    return pl.pallas_call(
        collect_kernel,
        in_specs=[pl.BlockSpec(memory_space=pltpu.SMEM), whole, whole],
        out_specs=[whole] * 3,
        out_shape=[jax.ShapeDtypeStruct((n, w), BF16) for w in (QW, HD, HD)],
        name="collect",
        cost_estimate=pl.CostEstimate(flops=0, bytes_accessed=7 * 10**6, transcendentals=0),
    )(sources, early, late)


def hop(x, pairs):
    return lax.ppermute(x, "mp", pairs)


def ring(w, n, first=()):
    up = [(i, (i + 1) % n) for i in range(n)]
    down = [(i, (i - 1) % n) for i in range(n)]
    a = b = w
    got = {0: w}
    for k in range(1, n // 2):
        a = hop(a, up)
        b = hop(b, down)
        if first and k == 1:
            b, *_ = lax.optimization_barrier((b, *first))
        got[n - k], got[k] = a, b
    m = w.shape[0] // 2
    k = n // 2
    got[k] = jnp.concatenate([hop(a[:m], up), hop(b[m:], down)], axis=0)
    return got


def local(q, k, v, grad_out, out_proj, lengths, offsets):
    n = lax.axis_size("mp")
    z = lax.axis_index("mp")
    core = lax.axis_index("c")
    me = lax.axis_index(("x", "y", "c"))
    width = grad_out.shape[1]
    own = lax.dynamic_slice(lengths, (me * SLOTS, 0), (SLOTS, lengths.shape[1]))
    segment, weight = doc_layout(own, BLOCK)
    ids = segment + 4 * jnp.arange(SLOTS, dtype=jnp.int32)[:, None]
    targets = (me + offsets) % RANKS
    sources = (me - offsets) % RANKS
    weighted = (grad_out.astype(F32) * weight.reshape(-1, 1)).astype(BF16).reshape(SLOTS, BLOCK, width)
    w0 = weighted[:, :HALF].reshape(-1, width)
    w1 = weighted[:, HALF:].reshape(-1, width)
    order = list(range(n))
    proj = {j: lax.dynamic_slice(out_proj, (0, ((z + j) % n) * width), (QW, width)) for j in order}
    return work(n, z, core, q, k, v, ids, targets, sources, proj, w0, w1)


def work(n, z, core, q, k, v, ids, targets, sources, proj, w0, w1):
    width = w0.shape[1]
    order = list(range(n))
    prep = id_views(ids)
    att0, att1, s00, s10, s11 = forward(q, k, v, *prep)
    got1 = ring(w1, n, prep)
    w0, _ = lax.optimization_barrier((w0, got1[n // 2 - 1]))
    got0 = ring(w0, n)
    walk = sorted(order, key=lambda j: min(j, n - j))

    def head_grad(got):
        total = None
        for j in walk:
            term = mm(got[j], proj[j], NT)
            total = term if total is None else total + term
            if j == walk[-1]:
                total = total.astype(BF16)
        return total

    sent1, dk, dv = backward(True, targets, head_grad(got1), att1, q, k, v, (s10, s11))
    back1 = lax.all_to_all(sent1, ("x", "y", "c"), split_axis=0, concat_axis=0, tiled=True)
    hg0, _ = lax.optimization_barrier((head_grad(got0), back1))
    sent0 = backward(False, targets, hg0, att0, q, k, v, (s00,), (dk, dv))
    back0 = lax.all_to_all(sent0, ("x", "y", "c"), split_axis=0, concat_axis=0, tiled=True)
    gq, gk, gv = collect(sources, back0, back1)

    mine = width // 4
    stack = jnp.zeros((n, 2, 2, mine, QW), BF16)
    for j in walk:
        x0 = got0[j]
        if min(j, n - j) > 1:
            x0, _ = lax.optimization_barrier((x0, sent0))
        part = (mm(got1[j], att1, TN) + mm(x0, att0, TN)).astype(BF16)
        stack = lax.dynamic_update_slice(stack, part.reshape(1, 2, 2, mine, QW), ((z + j) % n, 0, 0, 0, 0))
    keep = lax.dynamic_index_in_dim(stack, core, axis=2, keepdims=False)
    give = lax.dynamic_index_in_dim(stack, 1 - core, axis=2, keepdims=False)
    taken = lax.ppermute(give, "c", [(0, 1), (1, 0)])
    pair = (keep.astype(F32) + taken.astype(F32)).astype(BF16).reshape(2 * n, mine, QW)
    spread = lax.all_to_all(pair, ("x", "y"), split_axis=0, concat_axis=0, tiled=True)
    grad_proj = jnp.sum(spread.astype(F32), axis=0)
    return gq, gk, gv, grad_proj


def solution(mesh):
    fine = Mesh(mesh.devices.reshape(4, 4, 2, 8), ("x", "y", "c", "mp"))
    rows = P(("x", "y", "c"), "mp")
    return jax.shard_map(
        local,
        mesh=fine,
        in_specs=(rows, rows, rows, rows, P("mp", None), P(), P()),
        out_specs=(rows, rows, rows, rows),
        check_vma=False,
    )
```

```python
import functools

import jax
import jax.numpy as jnp
from jax import lax
from jax.experimental import pallas as pl
from jax.experimental.pallas import tpu as pltpu
from jax.sharding import Mesh, PartitionSpec as P


HEADS = 40
KVH = 8
HD = 128
GROUP = HEADS // KVH
BLOCK = 64
HALF = BLOCK // 2
SLOTS = 16
RANKS = 32
QW = GROUP * HD
SENT = QW + 2 * HD
PACK = 4
ROWS = PACK * HALF
SCALE = HD**-0.5
F32 = jnp.float32
BF16 = jnp.bfloat16

NT = (((1,), (1,)), ((), ()))
TN = (((0,), (0,)), ((), ()))
NN = (((1,), (0,)), ((), ()))


def mm(a, b, dims):
    return lax.dot_general(a, b, dims, preferred_element_type=F32)


def doc_layout(lengths, block_len):
    doc_ends = jnp.cumsum(lengths, axis=1)
    positions = jnp.arange(block_len, dtype=jnp.int32)
    segment = jnp.sum((doc_ends[:, None, :] <= positions[None, :, None]).astype(jnp.int32), axis=2)
    doc_ids = jnp.arange(lengths.shape[1], dtype=jnp.int32)
    onehot_doc = segment[:, :, None] == doc_ids[None, None, :]
    own_length = jnp.sum(jnp.where(onehot_doc, lengths[:, None, :], 0), axis=2)
    return segment, 1.0 / own_length.astype(F32)


def halves(ref):
    x = ref[...]
    return x[:, :HALF].reshape(ROWS, x.shape[2]), x[:, HALF:].reshape(ROWS, x.shape[2])


def lower_mask():
    r = lax.broadcasted_iota(jnp.int32, (ROWS, ROWS), 0)
    c = lax.broadcasted_iota(jnp.int32, (ROWS, ROWS), 1)
    return c <= r


def forward_kernel(q_ref, k_ref, v_ref, rows0_ref, rows1_ref, cols0_ref, cols1_ref, att0_ref, att1_ref, s00_ref, s10_ref, s11_ref):
    q0, q1 = halves(q_ref)
    k0, k1 = halves(k_ref)
    v0, v1 = halves(v_ref)
    rows0, rows1 = rows0_ref[...], rows1_ref[...]
    cols0, cols1 = cols0_ref[0], cols1_ref[0]
    low = lower_mask()
    m00 = (rows0 == cols0) & low
    m10 = rows1 == cols0
    m11 = (rows1 == cols1) & low
    for h in range(GROUP):
        cut = slice(h * HD, (h + 1) * HD)
        qh = q0[:, cut]
        s = jnp.where(m00, mm(qh, k0, NT) * SCALE, -1e30)
        e = jnp.where(m00, jnp.exp(s - jnp.max(s, axis=1, keepdims=True)), 0.0)
        soft = e / jnp.sum(e, axis=1, keepdims=True)
        s00_ref[0, h] = soft
        att0_ref[:, cut] = mm(soft.astype(BF16), v0, NN).astype(BF16)
        qh = q1[:, cut]
        s0 = jnp.where(m10, mm(qh, k0, NT) * SCALE, -1e30)
        s1 = jnp.where(m11, mm(qh, k1, NT) * SCALE, -1e30)
        top = jnp.maximum(jnp.max(s0, axis=1, keepdims=True), jnp.max(s1, axis=1, keepdims=True))
        e0 = jnp.where(m10, jnp.exp(s0 - top), 0.0)
        e1 = jnp.where(m11, jnp.exp(s1 - top), 0.0)
        total = jnp.sum(e0, axis=1, keepdims=True) + jnp.sum(e1, axis=1, keepdims=True)
        soft0, soft1 = e0 / total, e1 / total
        s10_ref[0, h] = soft0
        s11_ref[0, h] = soft1
        att1_ref[:, cut] = (mm(soft0.astype(BF16), v0, NN) + mm(soft1.astype(BF16), v1, NN)).astype(BF16)


def id_views(ids):
    half = ids.reshape(SLOTS, 2, HALF)
    id0, id1 = half[:, 0].reshape(-1), half[:, 1].reshape(-1)
    steps = SLOTS // PACK
    return id0[:, None], id1[:, None], id0.reshape(steps, 1, ROWS), id1.reshape(steps, 1, ROWS)


def forward(q, k, v, *id_arrays):
    steps = SLOTS // PACK
    wide = lambda n: pl.BlockSpec((PACK, BLOCK, n), lambda i: (i, 0, 0))
    rows = pl.BlockSpec((ROWS, 1), lambda i: (i, 0))
    cols = pl.BlockSpec((1, 1, ROWS), lambda i: (i, 0, 0))
    att = pl.BlockSpec((ROWS, QW), lambda i: (i, 0))
    soft = pl.BlockSpec((1, GROUP, ROWS, ROWS), lambda i: (i, 0, 0, 0))
    return pl.pallas_call(
        forward_kernel,
        grid=(steps,),
        in_specs=[wide(QW), wide(HD), wide(HD), rows, rows, cols, cols],
        out_specs=[att, att, soft, soft, soft],
        out_shape=[jax.ShapeDtypeStruct((SLOTS * HALF, QW), BF16)] * 2
        + [jax.ShapeDtypeStruct((steps, GROUP, ROWS, ROWS), F32)] * 3,
        name="forward",
        cost_estimate=pl.CostEstimate(flops=10**9, bytes_accessed=10**7, transcendentals=10**6),
    )(
        q.reshape(SLOTS, BLOCK, QW),
        k.reshape(SLOTS, BLOCK, HD),
        v.reshape(SLOTS, BLOCK, HD),
        *id_arrays,
    )


def put(send_ref, tgt_ref, first, value, lo):
    for j in range(PACK):
        send_ref[tgt_ref[first + j], :, lo : lo + value.shape[1]] = value[j * HALF : (j + 1) * HALF].astype(BF16)


def late_kernel(tgt_ref, hg_ref, att_ref, q_ref, k_ref, v_ref, s10_ref, s11_ref, send_ref, dk_ref, dv_ref):
    first = pl.program_id(0) * PACK
    q1 = halves(q_ref)[1]
    k0, k1 = halves(k_ref)
    v0, v1 = halves(v_ref)
    dk0 = dk1 = dv0 = dv1 = jnp.zeros((ROWS, HD), F32)
    for h in range(GROUP):
        cut = slice(h * HD, (h + 1) * HD)
        g, qh = hg_ref[:, cut], q1[:, cut]
        soft0, soft1 = s10_ref[0, h], s11_ref[0, h]
        dot = jnp.sum(g.astype(F32) * att_ref[:, cut].astype(F32), axis=1, keepdims=True)
        d0 = (soft0 * (mm(g, v0, NT) - dot)).astype(BF16)
        d1 = (soft1 * (mm(g, v1, NT) - dot)).astype(BF16)
        put(send_ref, tgt_ref, first, (mm(d0, k0, NN) + mm(d1, k1, NN)) * SCALE, h * HD)
        dk0 += mm(d0, qh, TN)
        dk1 += mm(d1, qh, TN)
        dv0 += mm(soft0.astype(BF16), g, TN)
        dv1 += mm(soft1.astype(BF16), g, TN)
    put(send_ref, tgt_ref, first, dk1 * SCALE, QW)
    put(send_ref, tgt_ref, first, dv1, QW + HD)
    dk_ref[...] = dk0
    dv_ref[...] = dv0


def early_kernel(tgt_ref, hg_ref, att_ref, q_ref, k_ref, v_ref, s00_ref, dk_ref, dv_ref, send_ref):
    first = pl.program_id(0) * PACK
    q0 = halves(q_ref)[0]
    k0 = halves(k_ref)[0]
    v0 = halves(v_ref)[0]
    dk0, dv0 = dk_ref[...], dv_ref[...]
    for h in range(GROUP):
        cut = slice(h * HD, (h + 1) * HD)
        g, qh = hg_ref[:, cut], q0[:, cut]
        soft0 = s00_ref[0, h]
        dot = jnp.sum(g.astype(F32) * att_ref[:, cut].astype(F32), axis=1, keepdims=True)
        d0 = (soft0 * (mm(g, v0, NT) - dot)).astype(BF16)
        put(send_ref, tgt_ref, first, mm(d0, k0, NN) * SCALE, h * HD)
        dk0 += mm(d0, qh, TN)
        dv0 += mm(soft0.astype(BF16), g, TN)
    put(send_ref, tgt_ref, first, dk0 * SCALE, QW)
    put(send_ref, tgt_ref, first, dv0, QW + HD)


def backward(late, targets, hg, att, q, k, v, softs, carry=()):
    wide = lambda n: pl.BlockSpec((PACK, BLOCK, n), lambda i, t: (i, 0, 0))
    att_spec = pl.BlockSpec((ROWS, QW), lambda i, t: (i, 0))
    soft = pl.BlockSpec((1, GROUP, ROWS, ROWS), lambda i, t: (i, 0, 0, 0))
    narrow = pl.BlockSpec((ROWS, HD), lambda i, t: (i, 0))
    send = pl.BlockSpec((RANKS, HALF, SENT), lambda i, t: (0, 0, 0))
    send_shape = jax.ShapeDtypeStruct((RANKS, HALF, SENT), BF16)
    part = jax.ShapeDtypeStruct((SLOTS * HALF, HD), F32)
    return pl.pallas_call(
        late_kernel if late else early_kernel,
        grid_spec=pltpu.PrefetchScalarGridSpec(
            num_scalar_prefetch=1,
            grid=(SLOTS // PACK,),
            in_specs=[att_spec, att_spec, wide(QW), wide(HD), wide(HD)] + [soft] * len(softs) + [narrow] * len(carry),
            out_specs=[send, narrow, narrow] if late else send,
        ),
        out_shape=[send_shape, part, part] if late else send_shape,
        name="late" if late else "early",
        cost_estimate=pl.CostEstimate(flops=10**9, bytes_accessed=10**7, transcendentals=0),
    )(
        targets,
        hg,
        att,
        q.reshape(SLOTS, BLOCK, QW),
        k.reshape(SLOTS, BLOCK, HD),
        v.reshape(SLOTS, BLOCK, HD),
        *softs,
        *carry,
    )


def collect_kernel(src_ref, early_ref, late_ref, gq_ref, gk_ref, gv_ref):
    for s in range(SLOTS):
        for ref, lo in ((early_ref, s * BLOCK), (late_ref, s * BLOCK + HALF)):
            rows = pl.ds(lo, HALF)
            piece = ref[src_ref[s]]
            gq_ref[rows] = piece[:, :QW]
            gk_ref[rows] = piece[:, QW : QW + HD]
            gv_ref[rows] = piece[:, QW + HD :]


def collect(sources, early, late):
    n = SLOTS * BLOCK
    whole = pl.BlockSpec(memory_space=pltpu.VMEM)
    return pl.pallas_call(
        collect_kernel,
        in_specs=[pl.BlockSpec(memory_space=pltpu.SMEM), whole, whole],
        out_specs=[whole] * 3,
        out_shape=[jax.ShapeDtypeStruct((n, w), BF16) for w in (QW, HD, HD)],
        name="collect",
        cost_estimate=pl.CostEstimate(flops=0, bytes_accessed=7 * 10**6, transcendentals=0),
    )(sources, early, late)


def product_kernel(n, where_ref, *refs):
    late, early = refs[:n], refs[n : 2 * n]
    att1_ref, att0_ref, keep_ref, give_ref = refs[2 * n :]
    first = where_ref[n] == 0
    rows = keep_ref.shape[2]
    for j in range(n):
        part = mm(late[j][...], att1_ref[...], TN) + mm(early[j][...], att0_ref[...], TN)
        for b in range(2):
            even = part[2 * b * rows : (2 * b + 1) * rows]
            odd = part[(2 * b + 1) * rows : (2 * b + 2) * rows]
            keep_ref[where_ref[j], b] = jnp.where(first, even, odd).astype(BF16)
            give_ref[where_ref[j], b] = jnp.where(first, odd, even).astype(BF16)


def product(n, where, late, early, att1, att0):
    whole = pl.BlockSpec(memory_space=pltpu.VMEM)
    out = jax.ShapeDtypeStruct((n, 2, late[0].shape[1] // 4, QW), BF16)
    return pl.pallas_call(
        functools.partial(product_kernel, n),
        in_specs=[pl.BlockSpec(memory_space=pltpu.SMEM)] + [whole] * (2 * n + 2),
        out_specs=[whole] * 2,
        out_shape=[out] * 2,
        name="product",
        cost_estimate=pl.CostEstimate(flops=7 * 10**9, bytes_accessed=2 * 10**7, transcendentals=0),
    )(where, *late, *early, att1, att0)


def hop(x, pairs):
    return lax.ppermute(x, "mp", pairs)


def ring(w, n, first=()):
    up = [(i, (i + 1) % n) for i in range(n)]
    down = [(i, (i - 1) % n) for i in range(n)]
    a = b = w
    got = {0: w}
    for k in range(1, n // 2):
        a = hop(a, up)
        b = hop(b, down)
        if first and k == 1:
            b, *_ = lax.optimization_barrier((b, *first))
        got[n - k], got[k] = a, b
    m = w.shape[0] // 2
    k = n // 2
    got[k] = jnp.concatenate([hop(a[:m], up), hop(b[m:], down)], axis=0)
    return got


def local(q, k, v, grad_out, out_proj, lengths, offsets):
    n = lax.axis_size("mp")
    z = lax.axis_index("mp")
    core = lax.axis_index("c")
    me = lax.axis_index(("x", "y", "c"))
    width = grad_out.shape[1]
    own = lax.dynamic_slice(lengths, (me * SLOTS, 0), (SLOTS, lengths.shape[1]))
    segment, weight = doc_layout(own, BLOCK)
    ids = segment + 4 * jnp.arange(SLOTS, dtype=jnp.int32)[:, None]
    targets = (me + offsets) % RANKS
    sources = (me - offsets) % RANKS
    weighted = (grad_out.astype(F32) * weight.reshape(-1, 1)).astype(BF16).reshape(SLOTS, BLOCK, width)
    w0 = weighted[:, :HALF].reshape(-1, width)
    w1 = weighted[:, HALF:].reshape(-1, width)
    order = list(range(n))
    proj = {j: lax.dynamic_slice(out_proj, (0, ((z + j) % n) * width), (QW, width)) for j in order}
    return work(n, z, core, q, k, v, ids, targets, sources, proj, w0, w1)


def work(n, z, core, q, k, v, ids, targets, sources, proj, w0, w1):
    width = w0.shape[1]
    order = list(range(n))
    prep = id_views(ids)
    att0, att1, s00, s10, s11 = forward(q, k, v, *prep)
    got1 = ring(w1, n, prep)
    w0, _ = lax.optimization_barrier((w0, got1[n // 2 - 1]))
    got0 = ring(w0, n)
    walk = sorted(order, key=lambda j: min(j, n - j))

    def head_grad(got):
        total = None
        for j in walk:
            term = mm(got[j], proj[j], NT)
            total = term if total is None else total + term
            if j == walk[-1]:
                total = total.astype(BF16)
        return total

    sent1, dk, dv = backward(True, targets, head_grad(got1), att1, q, k, v, (s10, s11))
    back1 = lax.all_to_all(sent1, ("x", "y", "c"), split_axis=0, concat_axis=0, tiled=True)
    hg0, _ = lax.optimization_barrier((head_grad(got0), back1))
    sent0 = backward(False, targets, hg0, att0, q, k, v, (s00,), (dk, dv))
    back0 = lax.all_to_all(sent0, ("x", "y", "c"), split_axis=0, concat_axis=0, tiled=True)
    gq, gk, gv = collect(sources, back0, back1)

    mine = width // 4
    where = jnp.concatenate([(z + jnp.arange(n, dtype=jnp.int32)) % n, jnp.full((1,), core, jnp.int32)])
    keep, give = product(n, where, [got1[j] for j in order], [got0[j] for j in order], att1, att0)
    taken = lax.ppermute(give, "c", [(0, 1), (1, 0)])
    pair = (keep.astype(F32) + taken.astype(F32)).astype(BF16).reshape(2 * n, mine, QW)
    spread = lax.all_to_all(pair, ("x", "y"), split_axis=0, concat_axis=0, tiled=True)
    grad_proj = jnp.sum(spread.astype(F32), axis=0)
    return gq, gk, gv, grad_proj


def solution(mesh):
    fine = Mesh(mesh.devices.reshape(4, 4, 2, 8), ("x", "y", "c", "mp"))
    rows = P(("x", "y", "c"), "mp")
    return jax.shard_map(
        local,
        mesh=fine,
        in_specs=(rows, rows, rows, rows, P("mp", None), P(), P()),
        out_specs=(rows, rows, rows, rows),
        check_vma=False,
    )
```

```python
import functools

import jax
import jax.numpy as jnp
from jax import lax
from jax.experimental import pallas as pl
from jax.experimental.pallas import tpu as pltpu
from jax.sharding import Mesh, PartitionSpec as P


HEADS = 40
KVH = 8
HD = 128
GROUP = HEADS // KVH
BLOCK = 64
HALF = BLOCK // 2
SLOTS = 16
RANKS = 32
QW = GROUP * HD
SENT = QW + 2 * HD
PACK = 4
ROWS = PACK * HALF
SCALE = HD**-0.5
F32 = jnp.float32
BF16 = jnp.bfloat16

NT = (((1,), (1,)), ((), ()))
TN = (((0,), (0,)), ((), ()))
NN = (((1,), (0,)), ((), ()))


def mm(a, b, dims):
    return lax.dot_general(a, b, dims, preferred_element_type=F32)


def doc_layout(lengths, block_len):
    doc_ends = jnp.cumsum(lengths, axis=1)
    positions = jnp.arange(block_len, dtype=jnp.int32)
    segment = jnp.sum((doc_ends[:, None, :] <= positions[None, :, None]).astype(jnp.int32), axis=2)
    doc_ids = jnp.arange(lengths.shape[1], dtype=jnp.int32)
    onehot_doc = segment[:, :, None] == doc_ids[None, None, :]
    own_length = jnp.sum(jnp.where(onehot_doc, lengths[:, None, :], 0), axis=2)
    return segment, 1.0 / own_length.astype(F32)


def halves(ref):
    x = ref[...]
    return x[:, :HALF].reshape(ROWS, x.shape[2]), x[:, HALF:].reshape(ROWS, x.shape[2])


def lower_mask():
    r = lax.broadcasted_iota(jnp.int32, (ROWS, ROWS), 0)
    c = lax.broadcasted_iota(jnp.int32, (ROWS, ROWS), 1)
    return c <= r


def forward_kernel(q_ref, k_ref, v_ref, rows0_ref, rows1_ref, cols0_ref, cols1_ref, att0_ref, att1_ref, s00_ref, s10_ref, s11_ref):
    q0, q1 = halves(q_ref)
    k0, k1 = halves(k_ref)
    v0, v1 = halves(v_ref)
    rows0, rows1 = rows0_ref[...], rows1_ref[...]
    cols0, cols1 = cols0_ref[0], cols1_ref[0]
    low = lower_mask()
    m00 = (rows0 == cols0) & low
    m10 = rows1 == cols0
    m11 = (rows1 == cols1) & low
    for h in range(GROUP):
        cut = slice(h * HD, (h + 1) * HD)
        qh = q0[:, cut]
        s = jnp.where(m00, mm(qh, k0, NT) * SCALE, -1e30)
        e = jnp.where(m00, jnp.exp(s - jnp.max(s, axis=1, keepdims=True)), 0.0)
        soft = e / jnp.sum(e, axis=1, keepdims=True)
        s00_ref[0, h] = soft
        att0_ref[:, cut] = mm(soft.astype(BF16), v0, NN).astype(BF16)
        qh = q1[:, cut]
        s0 = jnp.where(m10, mm(qh, k0, NT) * SCALE, -1e30)
        s1 = jnp.where(m11, mm(qh, k1, NT) * SCALE, -1e30)
        top = jnp.maximum(jnp.max(s0, axis=1, keepdims=True), jnp.max(s1, axis=1, keepdims=True))
        e0 = jnp.where(m10, jnp.exp(s0 - top), 0.0)
        e1 = jnp.where(m11, jnp.exp(s1 - top), 0.0)
        total = jnp.sum(e0, axis=1, keepdims=True) + jnp.sum(e1, axis=1, keepdims=True)
        soft0, soft1 = e0 / total, e1 / total
        s10_ref[0, h] = soft0
        s11_ref[0, h] = soft1
        att1_ref[:, cut] = (mm(soft0.astype(BF16), v0, NN) + mm(soft1.astype(BF16), v1, NN)).astype(BF16)


def id_views(ids):
    half = ids.reshape(SLOTS, 2, HALF)
    id0, id1 = half[:, 0].reshape(-1), half[:, 1].reshape(-1)
    steps = SLOTS // PACK
    return id0[:, None], id1[:, None], id0.reshape(steps, 1, ROWS), id1.reshape(steps, 1, ROWS)


def forward(q, k, v, *id_arrays):
    steps = SLOTS // PACK
    wide = lambda n: pl.BlockSpec((PACK, BLOCK, n), lambda i: (i, 0, 0))
    rows = pl.BlockSpec((ROWS, 1), lambda i: (i, 0))
    cols = pl.BlockSpec((1, 1, ROWS), lambda i: (i, 0, 0))
    att = pl.BlockSpec((ROWS, QW), lambda i: (i, 0))
    soft = pl.BlockSpec((1, GROUP, ROWS, ROWS), lambda i: (i, 0, 0, 0))
    return pl.pallas_call(
        forward_kernel,
        grid=(steps,),
        in_specs=[wide(QW), wide(HD), wide(HD), rows, rows, cols, cols],
        out_specs=[att, att, soft, soft, soft],
        out_shape=[jax.ShapeDtypeStruct((SLOTS * HALF, QW), BF16)] * 2
        + [jax.ShapeDtypeStruct((steps, GROUP, ROWS, ROWS), F32)] * 3,
        name="forward",
        cost_estimate=pl.CostEstimate(flops=10**9, bytes_accessed=10**7, transcendentals=10**6),
    )(
        q.reshape(SLOTS, BLOCK, QW),
        k.reshape(SLOTS, BLOCK, HD),
        v.reshape(SLOTS, BLOCK, HD),
        *id_arrays,
    )


def put(send_ref, tgt_ref, first, value, lo):
    for j in range(PACK):
        send_ref[tgt_ref[first + j], :, lo : lo + value.shape[1]] = value[j * HALF : (j + 1) * HALF].astype(BF16)


def late_kernel(tgt_ref, hg_ref, att_ref, q_ref, k_ref, v_ref, s10_ref, s11_ref, send_ref, dk_ref, dv_ref):
    first = pl.program_id(0) * PACK
    q1 = halves(q_ref)[1]
    k0, k1 = halves(k_ref)
    v0, v1 = halves(v_ref)
    dk0 = dk1 = dv0 = dv1 = jnp.zeros((ROWS, HD), F32)
    for h in range(GROUP):
        cut = slice(h * HD, (h + 1) * HD)
        g, qh = hg_ref[:, cut], q1[:, cut]
        soft0, soft1 = s10_ref[0, h], s11_ref[0, h]
        dot = jnp.sum(g.astype(F32) * att_ref[:, cut].astype(F32), axis=1, keepdims=True)
        d0 = (soft0 * (mm(g, v0, NT) - dot)).astype(BF16)
        d1 = (soft1 * (mm(g, v1, NT) - dot)).astype(BF16)
        put(send_ref, tgt_ref, first, (mm(d0, k0, NN) + mm(d1, k1, NN)) * SCALE, h * HD)
        dk0 += mm(d0, qh, TN)
        dk1 += mm(d1, qh, TN)
        dv0 += mm(soft0.astype(BF16), g, TN)
        dv1 += mm(soft1.astype(BF16), g, TN)
    put(send_ref, tgt_ref, first, dk1 * SCALE, QW)
    put(send_ref, tgt_ref, first, dv1, QW + HD)
    dk_ref[...] = dk0
    dv_ref[...] = dv0


def early_kernel(tgt_ref, hg_ref, att_ref, q_ref, k_ref, v_ref, s00_ref, dk_ref, dv_ref, send_ref):
    first = pl.program_id(0) * PACK
    q0 = halves(q_ref)[0]
    k0 = halves(k_ref)[0]
    v0 = halves(v_ref)[0]
    dk0, dv0 = dk_ref[...], dv_ref[...]
    for h in range(GROUP):
        cut = slice(h * HD, (h + 1) * HD)
        g, qh = hg_ref[:, cut], q0[:, cut]
        soft0 = s00_ref[0, h]
        dot = jnp.sum(g.astype(F32) * att_ref[:, cut].astype(F32), axis=1, keepdims=True)
        d0 = (soft0 * (mm(g, v0, NT) - dot)).astype(BF16)
        put(send_ref, tgt_ref, first, mm(d0, k0, NN) * SCALE, h * HD)
        dk0 += mm(d0, qh, TN)
        dv0 += mm(soft0.astype(BF16), g, TN)
    put(send_ref, tgt_ref, first, dk0 * SCALE, QW)
    put(send_ref, tgt_ref, first, dv0, QW + HD)


def backward(late, targets, hg, att, q, k, v, softs, carry=()):
    wide = lambda n: pl.BlockSpec((PACK, BLOCK, n), lambda i, t: (i, 0, 0))
    att_spec = pl.BlockSpec((ROWS, QW), lambda i, t: (i, 0))
    soft = pl.BlockSpec((1, GROUP, ROWS, ROWS), lambda i, t: (i, 0, 0, 0))
    narrow = pl.BlockSpec((ROWS, HD), lambda i, t: (i, 0))
    send = pl.BlockSpec((RANKS, HALF, SENT), lambda i, t: (0, 0, 0))
    send_shape = jax.ShapeDtypeStruct((RANKS, HALF, SENT), BF16)
    part = jax.ShapeDtypeStruct((SLOTS * HALF, HD), F32)
    return pl.pallas_call(
        late_kernel if late else early_kernel,
        grid_spec=pltpu.PrefetchScalarGridSpec(
            num_scalar_prefetch=1,
            grid=(SLOTS // PACK,),
            in_specs=[att_spec, att_spec, wide(QW), wide(HD), wide(HD)] + [soft] * len(softs) + [narrow] * len(carry),
            out_specs=[send, narrow, narrow] if late else send,
        ),
        out_shape=[send_shape, part, part] if late else send_shape,
        name="late" if late else "early",
        cost_estimate=pl.CostEstimate(flops=10**9, bytes_accessed=10**7, transcendentals=0),
    )(
        targets,
        hg,
        att,
        q.reshape(SLOTS, BLOCK, QW),
        k.reshape(SLOTS, BLOCK, HD),
        v.reshape(SLOTS, BLOCK, HD),
        *softs,
        *carry,
    )


def collect_kernel(src_ref, early_ref, late_ref, gq_ref, gk_ref, gv_ref):
    for s in range(SLOTS):
        for ref, lo in ((early_ref, s * BLOCK), (late_ref, s * BLOCK + HALF)):
            rows = pl.ds(lo, HALF)
            piece = ref[src_ref[s]]
            gq_ref[rows] = piece[:, :QW]
            gk_ref[rows] = piece[:, QW : QW + HD]
            gv_ref[rows] = piece[:, QW + HD :]


def collect(sources, early, late):
    n = SLOTS * BLOCK
    whole = pl.BlockSpec(memory_space=pltpu.VMEM)
    return pl.pallas_call(
        collect_kernel,
        in_specs=[pl.BlockSpec(memory_space=pltpu.SMEM), whole, whole],
        out_specs=[whole] * 3,
        out_shape=[jax.ShapeDtypeStruct((n, w), BF16) for w in (QW, HD, HD)],
        name="collect",
        cost_estimate=pl.CostEstimate(flops=0, bytes_accessed=7 * 10**6, transcendentals=0),
    )(sources, early, late)


def product_kernel(n, where_ref, *refs):
    late, early = refs[:n], refs[n : 2 * n]
    att1_ref, att0_ref, keep_ref, give_ref = refs[2 * n :]
    first = where_ref[n] == 0
    rows = keep_ref.shape[2]
    for j in range(n):
        part = mm(late[j][...], att1_ref[...], TN) + mm(early[j][...], att0_ref[...], TN)
        for b in range(2):
            even = part[2 * b * rows : (2 * b + 1) * rows]
            odd = part[(2 * b + 1) * rows : (2 * b + 2) * rows]
            keep_ref[where_ref[j], b] = jnp.where(first, even, odd).astype(BF16)
            give_ref[where_ref[j], b] = jnp.where(first, odd, even).astype(BF16)


def product(n, where, late, early, att1, att0):
    whole = pl.BlockSpec(memory_space=pltpu.VMEM)
    out = jax.ShapeDtypeStruct((n, 2, late[0].shape[1] // 4, QW), BF16)
    return pl.pallas_call(
        functools.partial(product_kernel, n),
        in_specs=[pl.BlockSpec(memory_space=pltpu.SMEM)] + [whole] * (2 * n + 2),
        out_specs=[whole] * 2,
        out_shape=[out] * 2,
        name="product",
        cost_estimate=pl.CostEstimate(flops=7 * 10**9, bytes_accessed=2 * 10**7, transcendentals=0),
    )(where, *late, *early, att1, att0)


def partial_kernel(n, where_ref, *refs):
    proj_ref, out_ref = refs[n:]
    half = out_ref.shape[0] // 2
    width = refs[0].shape[1]

    def step(i, carry):
        rows = pl.ds(pl.multiple_of(i * half, half), half)
        total = jnp.zeros((half, out_ref.shape[1]), F32)
        for j in range(n):
            cols = pl.ds(pl.multiple_of(where_ref[j] * width, width), width)
            total += mm(refs[j][rows, :], proj_ref[:, cols], NT)
        out_ref[rows, :] = total
        return carry

    lax.fori_loop(0, 2, step, 0)


def partial_grad(where, slices, proj):
    n = len(slices)
    whole = pl.BlockSpec(memory_space=pltpu.VMEM)
    return pl.pallas_call(
        functools.partial(partial_kernel, n),
        in_specs=[pl.BlockSpec(memory_space=pltpu.SMEM)] + [whole] * (n + 1),
        out_specs=whole,
        out_shape=jax.ShapeDtypeStruct((slices[0].shape[0], QW), F32),
        name="partial_grad",
        cost_estimate=pl.CostEstimate(flops=n * 4 * 10**8, bytes_accessed=10**7, transcendentals=0),
    )(where, *slices, proj)


def hop(x, pairs):
    return lax.ppermute(x, "mp", pairs)


def ring(w, n, first=()):
    up = [(i, (i + 1) % n) for i in range(n)]
    down = [(i, (i - 1) % n) for i in range(n)]
    a = b = w
    got = {0: w}
    for k in range(1, n // 2):
        a = hop(a, up)
        b = hop(b, down)
        if first and k == 1:
            b, *_ = lax.optimization_barrier((b, *first))
        got[n - k], got[k] = a, b
    m = w.shape[0] // 2
    k = n // 2
    got[k] = jnp.concatenate([hop(a[:m], up), hop(b[m:], down)], axis=0)
    return got


def local(q, k, v, grad_out, out_proj, lengths, offsets):
    n = lax.axis_size("mp")
    z = lax.axis_index("mp")
    core = lax.axis_index("c")
    me = lax.axis_index(("x", "y", "c"))
    width = grad_out.shape[1]
    own = lax.dynamic_slice(lengths, (me * SLOTS, 0), (SLOTS, lengths.shape[1]))
    segment, weight = doc_layout(own, BLOCK)
    ids = segment + 4 * jnp.arange(SLOTS, dtype=jnp.int32)[:, None]
    targets = (me + offsets) % RANKS
    sources = (me - offsets) % RANKS
    weighted = (grad_out.astype(F32) * weight.reshape(-1, 1)).astype(BF16).reshape(SLOTS, BLOCK, width)
    w0 = weighted[:, :HALF].reshape(-1, width)
    w1 = weighted[:, HALF:].reshape(-1, width)
    order = list(range(n))
    proj = {j: lax.dynamic_slice(out_proj, (0, ((z + j) % n) * width), (QW, width)) for j in order}
    return work(n, z, core, q, k, v, ids, targets, sources, out_proj, proj, w0, w1)


def work(n, z, core, q, k, v, ids, targets, sources, out_proj, proj, w0, w1):
    width = w0.shape[1]
    order = list(range(n))
    prep = id_views(ids)
    att0, att1, s00, s10, s11 = forward(q, k, v, *prep)
    got1 = ring(w1, n, prep)
    w0, _ = lax.optimization_barrier((w0, got1[n // 2 - 1]))
    got0 = ring(w0, n)
    walk = sorted(order, key=lambda j: min(j, n - j))

    def head_grad(got, lead):
        near = walk[:lead]
        total = partial_grad((z + jnp.array(near, jnp.int32)) % n, [got[j] for j in near], out_proj)
        for j in walk[lead:]:
            total = total + mm(got[j], proj[j], NT)
            if j == walk[-1]:
                total = total.astype(BF16)
        return total

    sent1, dk, dv = backward(True, targets, head_grad(got1, 7), att1, q, k, v, (s10, s11))
    back1 = lax.all_to_all(sent1, ("x", "y", "c"), split_axis=0, concat_axis=0, tiled=True)
    hg0 = head_grad(got0, 7)
    sent0 = backward(False, targets, hg0, att0, q, k, v, (s00,), (dk, dv))
    back0 = lax.all_to_all(sent0, ("x", "y", "c"), split_axis=0, concat_axis=0, tiled=True)
    gq, gk, gv = collect(sources, back0, back1)

    mine = width // 4
    where = jnp.concatenate([(z + jnp.arange(n, dtype=jnp.int32)) % n, jnp.full((1,), core, jnp.int32)])
    keep, give = product(n, where, [got1[j] for j in order], [got0[j] for j in order], att1, att0)
    taken = lax.ppermute(give, "c", [(0, 1), (1, 0)])
    pair = (keep.astype(F32) + taken.astype(F32)).astype(BF16).reshape(2 * n, mine, QW)
    spread = lax.all_to_all(pair, ("x", "y"), split_axis=0, concat_axis=0, tiled=True)
    grad_proj = jnp.sum(spread.astype(F32), axis=0)
    return gq, gk, gv, grad_proj


def solution(mesh):
    fine = Mesh(mesh.devices.reshape(4, 4, 2, 8), ("x", "y", "c", "mp"))
    rows = P(("x", "y", "c"), "mp")
    return jax.shard_map(
        local,
        mesh=fine,
        in_specs=(rows, rows, rows, rows, P("mp", None), P(), P()),
        out_specs=(rows, rows, rows, rows),
        check_vma=False,
    )
```
